256 devices in a mesh: layer: 16 (over y, z_hi, core), feat: 16 (over x, z_lo).
Axes of the slice: x: 4, y: 4, z: 8 (z_hi: 2, z_lo: 4; z = z_hi * 4 + z_lo), core: 2. Of those that a mesh axis runs over, the one named last changes fastest.
Arguments:
- acts: bfloat16 [16, 768, 1024], P('layer'), may hold values from -6 to 6
- targets: bfloat16 [16, 768, 1024], P('layer', 'feat'), may hold values from -6 to 6
- enc_weight: bfloat16 [16, 1024, 20480], P('layer', None, 'feat'), may hold values from -0.1875 to 0.1875
- enc_bias: float32 [16, 20480], P('layer', 'feat'), may hold values from -3 to 3
- dec_weight: bfloat16 [16, 20480, 2, 1024], P('layer', 'feat'), may hold values from -0.0390625 to 0.0390625
- dec_bias: float32 [16, 1024], P('layer'), may hold values from -3 to 3
Outputs:
- errors: float32 [16, 768, 1024], P('layer', 'feat')
- enc_grad: bfloat16 [16, 1024, 20480], P('layer', None, 'feat')
The draws below stay inside these ranges and needn't reach their ends.
All inputs are finite; a program needn't handle non-finite values.
Results may differ from the reference program's by a relative error of at most 0.006.
Values may be sent and summed in bfloat16 or wider, within the bound.
No kernel may reach another device: no remote copies, remote signals or barrier semaphores. Data moves between devices by JAX's collectives and lax.ppermute only.
A program may use at most 128 MiB of HBM per device.

```python
import jax
import jax.numpy as jnp
from jax import lax

D = 1024
F = 20480
TOK = 768
LAYERS = 16


def block_levels(stream_key, extent, pieces, low, high):
    def one(axis_at, blocks):
        heights = jax.random.uniform(jax.random.fold_in(jax.random.fold_in(stream_key, 6), axis_at), (blocks,), jnp.float32, low / len(pieces), high / len(pieces))
        return jnp.repeat(jnp.exp(heights), extent[axis_at] // blocks).reshape((-1,) + (1,) * (len(extent) - axis_at - 1))

    gain = one(*pieces[0])
    for cut in pieces[1:]:
        gain = gain * one(*cut)
    return gain


def gaussian(key, dims, width, bound, pieces=(), kind=jnp.bfloat16):
    array = width * jax.random.normal(key, dims, jnp.float32)
    if pieces:
        array = array * block_levels(key, dims, pieces, -0.22, 0.18)
    return jnp.clip(array, -bound, bound).astype(kind)


def setup_inputs(seed: int = 0) -> dict:
    arg_keys = jax.random.split(jax.random.key(seed), 7)
    acts = gaussian(arg_keys[0], (LAYERS, TOK, D), 1.0, 6.0, ((0, 16),))
    targets = gaussian(arg_keys[1], (LAYERS, TOK, D), 1.0, 6.0, ((0, 16), (1, 16)))
    enc_weight = gaussian(arg_keys[2], (LAYERS, D, F), D ** -0.5, 0.1875, ((0, 16), (2, 16)))
    enc_bias = gaussian(arg_keys[3], (LAYERS, F), 0.5, 3.0, ((0, 16), (1, 16)), jnp.float32)
    dec_weight = gaussian(arg_keys[4], (LAYERS, F, 2, D), F ** -0.5, 0.0390625, ((0, 16), (1, 16)))
    dec_bias = gaussian(arg_keys[5], (LAYERS, D), 0.5, 3.0, ((0, 16),), jnp.float32)
    return {"acts": acts, "targets": targets, "enc_weight": enc_weight, "enc_bias": enc_bias, "dec_weight": dec_weight, "dec_bias": dec_bias}


def forward_layer(item):
    inputs, weight, bias, decoder = item
    pre = jnp.dot(inputs, weight, preferred_element_type=jnp.float32) + bias
    latent = (jax.nn.softplus(4.0 * pre) * 0.25).astype(jnp.bfloat16)
    own = jnp.dot(latent, decoder[:, 0, :], preferred_element_type=jnp.float32)
    later = jnp.dot(latent, decoder[:, 1, :], preferred_element_type=jnp.float32)
    return pre, own, later


def reference(acts, targets, enc_weight, enc_bias, dec_weight, dec_bias):
    pres, owns, laters = lax.map(forward_layer, (acts, enc_weight, enc_bias, dec_weight))
    carried = jnp.concatenate([jnp.zeros_like(laters[:1]), laters[:-1]], axis=0)
    errors = owns + carried + dec_bias[:, None, :] - targets.astype(jnp.float32)
    err_half = errors.astype(jnp.bfloat16)
    following = jnp.concatenate([err_half[1:], jnp.zeros_like(err_half[:1])], axis=0)
    scale = acts.shape[1] ** -0.5

    def backward_layer(item):
        inputs, pre, decoder, first, second = item
        grad_latent = lax.dot_general(first, decoder[:, 0, :], (((1,), (1,)), ((), ())), preferred_element_type=jnp.float32)
        grad_latent = grad_latent + lax.dot_general(second, decoder[:, 1, :], (((1,), (1,)), ((), ())), preferred_element_type=jnp.float32)
        grad_pre = (grad_latent * jax.nn.sigmoid(4.0 * pre)).astype(jnp.bfloat16)
        total = lax.dot_general(inputs, grad_pre, (((0,), (0,)), ((), ())), preferred_element_type=jnp.float32)
        return (total * scale).astype(jnp.bfloat16)

    enc_grad = lax.map(backward_layer, (acts, pres, dec_weight, err_half, following))
    return errors, enc_grad
```

```python
import jax
import jax.numpy as jnp
from jax import lax
from jax.sharding import Mesh
from jax.sharding import PartitionSpec as P

FEAT = ("feat_0", "feat_1")
MAIN_CUTS = 2


def summed_pieces(total, axis):
    peers = lax.axis_size(axis)
    rows = total.shape[0] // peers
    pieces = total.reshape(peers, rows, total.shape[1])
    pieces = lax.all_to_all(pieces, axis, 0, 0, tiled=True)
    return jnp.sum(pieces.astype(jnp.float32), axis=0)


def reduced(total):
    part = summed_pieces(total, FEAT[0]).astype(jnp.bfloat16)
    return summed_pieces(part, FEAT[1])


def gathered_over(value, axis):
    peers = lax.axis_size(axis)
    copies = jnp.broadcast_to(value[None], (peers, *value.shape))
    tiles = lax.all_to_all(copies, axis, 0, 0, tiled=True)
    return tiles.reshape(peers * value.shape[0], value.shape[1])


def gathered(value):
    return gathered_over(gathered_over(value, FEAT[1]), FEAT[0])


def on_chip(value):
    layers = lax.axis_size("layer")
    return lax.ppermute(value, "layer", [(i, i ^ 1) for i in range(layers)])


def across_chips(value):
    layers = lax.axis_size("layer")
    pairs = [(i, i + 1) for i in range(1, layers - 1, 2)]
    return lax.ppermute(value, "layer", pairs + [(j, i) for i, j in pairs])


def dot(a, b):
    return jnp.dot(a, b, preferred_element_type=jnp.float32)


def contract_width(errs, decoder):
    return lax.dot_general(
        errs, decoder, (((1,), (1,)), ((), ())), preferred_element_type=jnp.float32
    )


def local(acts, targets, enc_weight, enc_bias, dec_weight, dec_bias):
    inputs = acts[0]
    weight = enc_weight[0]
    bias = enc_bias[0]
    decoder = dec_weight[0]
    tokens, width = inputs.shape
    half = width // 2
    layer = lax.axis_index("layer")
    first = layer % 2 == 0
    ends = layer == lax.axis_size("layer") - 1

    offset = dec_bias[0] - targets[0].astype(jnp.float32)
    peer_offset = on_chip(offset[:, :half])

    pre = dot(inputs, weight) + bias
    latent = (jax.nn.softplus(4.0 * pre) * 0.25).astype(jnp.bfloat16)
    deriv = jax.nn.sigmoid(4.0 * pre)

    main = jnp.where(first, decoder[:, 0, :], decoder[:, 1, :])
    keep = jnp.where(first, decoder[:, 1, :half], decoder[:, 0, half:])
    give = jnp.where(first, decoder[:, 1, half:], decoder[:, 0, :half])
    main, keep, give = lax.optimization_barrier((main, keep, give))

    cut = width // MAIN_CUTS
    cuts = [slice(i * cut, (i + 1) * cut) for i in range(MAIN_CUTS)]
    sums = [reduced(dot(latent, main[:, c]).astype(jnp.bfloat16)) for c in cuts]
    given = on_chip(dot(latent, give).astype(jnp.bfloat16))
    shared = dot(latent, keep) + given.astype(jnp.float32)
    shared = reduced(shared.astype(jnp.bfloat16))

    shared = shared + jnp.where(first, peer_offset, offset[:, half:])
    shared_rows = gathered(shared.astype(jnp.bfloat16))
    other_rows = on_chip(shared_rows)
    other = on_chip(shared)

    mains = []
    rows = []
    for c, part in zip(cuts, sums):
        part = part + jnp.where(first, offset[:, c], 0.0)
        part = part + across_chips(part.astype(jnp.bfloat16)).astype(jnp.float32)
        mains.append(part)
        rows.append(gathered(jnp.where(ends, 0.0, part).astype(jnp.bfloat16)))

    errors = jnp.where(
        first, jnp.concatenate(mains, 1), jnp.concatenate([other, shared], 1)
    )

    grad_latent = contract_width(shared_rows, keep) + contract_width(other_rows, give)
    for c, block in zip(cuts, rows):
        grad_latent = grad_latent + contract_width(block, main[:, c])
    grad_pre = (grad_latent * deriv).astype(jnp.bfloat16)
    total = lax.dot_general(
        inputs, grad_pre, (((0,), (0,)), ((), ())), preferred_element_type=jnp.float32
    )
    enc_grad = (total * tokens ** (-0.5)).astype(jnp.bfloat16)
    return (errors[None], enc_grad[None])


def solution(mesh):
    finer = Mesh(mesh.devices.reshape(mesh.shape["layer"], 4, 4), ("layer", *FEAT))
    in_specs = (
        P("layer", None, None),
        P("layer", FEAT, None),
        P("layer", None, FEAT),
        P("layer", FEAT),
        P("layer", FEAT, None, None),
        P("layer", None),
    )
    out_specs = (P("layer", FEAT, None), P("layer", None, FEAT))
    return jax.shard_map(local, mesh=finer, in_specs=in_specs, out_specs=out_specs, check_vma=False)
```

```python
import jax
import jax.numpy as jnp
from jax import lax
from jax.experimental import pallas as pl
from jax.experimental.pallas import tpu as pltpu
from jax.sharding import Mesh
from jax.sharding import PartitionSpec as P

FEAT = ("feat_0", "feat_1")
SIDE = 4
HIGH = jnp.float32
LOW = jnp.bfloat16


def exchanged(piece, axis, step):
    return lax.ppermute(piece, axis, [(i, i ^ step) for i in range(SIDE)])


def after(value, *others):
    return lax.optimization_barrier((value, *others))[0]


def turned_kernel(places, blocks, out):
    for i in range(SIDE * SIDE):
        out[i] = blocks[places[i]]


def turned(array, places):
    blocks = array.reshape(SIDE * SIDE, -1, array.shape[1])
    out = pl.pallas_call(
        turned_kernel,
        in_specs=[
            pl.BlockSpec(memory_space=pltpu.SMEM),
            pl.BlockSpec(memory_space=pltpu.VMEM),
        ],
        out_specs=pl.BlockSpec(memory_space=pltpu.VMEM),
        out_shape=jax.ShapeDtypeStruct(blocks.shape, blocks.dtype),
        name="turned",
    )(places, blocks)
    return out.reshape(array.shape)


def summed_pieces(pieces, axis, *before):
    parts = [exchanged(pieces[step], axis, step) for step in range(1, SIDE)]
    total = after(pieces[0], *before).astype(HIGH)
    for part in parts:
        total = total + part.astype(HIGH)
    return total


def row_pieces(array):
    rows = array.shape[0] // SIDE
    return [array[i * rows : (i + 1) * rows] for i in range(SIDE)]


def gathered_over(value, axis):
    tiles = [value] + [exchanged(value, axis, step) for step in range(1, SIDE)]
    return jnp.concatenate(tiles, 0)


def on_chip(value):
    layers = lax.axis_size("layer")
    return lax.ppermute(value, "layer", [(i, i ^ 1) for i in range(layers)])


def across_chips(value):
    layers = lax.axis_size("layer")
    pairs = [(i, i + 1) for i in range(1, layers - 1, 2)]
    return lax.ppermute(value, "layer", pairs + [(j, i) for i, j in pairs])


def dot(a, b):
    return jnp.dot(a, b, preferred_element_type=HIGH)


def contract_width(errs, decoder):
    return lax.dot_general(errs, decoder, (((1,), (1,)), ((), ())), preferred_element_type=HIGH)


def local(acts, targets, enc_weight, enc_bias, dec_weight, dec_bias):
    weight = enc_weight[0]
    bias = enc_bias[0]
    decoder = dec_weight[0]
    tokens, width = acts.shape[1:]
    half = width // 2
    layer = lax.axis_index("layer")
    first = layer % 2 == 0
    ends = layer == lax.axis_size("layer") - 1

    steps = jnp.arange(SIDE, dtype=jnp.int32)
    along = lax.axis_index(FEAT[0]) ^ steps
    across = lax.axis_index(FEAT[1]) ^ steps
    inputs = turned(acts[0], (along[:, None] * SIDE + across).reshape(-1))

    pre = dot(inputs, weight) + bias
    scaled = 4.0 * pre
    small = jnp.exp(-jnp.abs(scaled))
    latent = ((jnp.maximum(scaled, 0.0) + jnp.log1p(small)) * 0.25).astype(LOW)
    latent, pre = lax.optimization_barrier((latent, pre))

    main = after(jnp.where(first, decoder[:, 0, :], decoder[:, 1, :]))
    part = dot(latent, main).astype(LOW)
    part, latent, pre, decoder = lax.optimization_barrier((part, latent, pre, decoder))

    keep = jnp.where(first, decoder[:, 1, :half], decoder[:, 0, half:])
    give = jnp.where(first, decoder[:, 1, half:], decoder[:, 0, :half])
    keep, give = lax.optimization_barrier((keep, give))
    given = on_chip(dot(latent, give).astype(LOW))
    offset = dec_bias[0] - targets[0].astype(HIGH)
    peer_offset = on_chip(offset[:, :half])
    shared = (dot(latent, keep) + given.astype(HIGH)).astype(LOW)

    part = summed_pieces(row_pieces(part), FEAT[0], shared).astype(LOW)
    shared = summed_pieces(row_pieces(shared), FEAT[0], part).astype(LOW)
    deriv = after(jax.nn.sigmoid(4.0 * pre))
    part = summed_pieces(row_pieces(part), FEAT[1], shared)
    part = part + jnp.where(first, offset, 0.0)
    sent = part.astype(LOW)
    shared = summed_pieces(row_pieces(shared), FEAT[1], sent)
    shared = shared + jnp.where(first, peer_offset, offset[:, half:])
    shared_rows = shared.astype(LOW)
    part = after(part, shared_rows) + across_chips(sent).astype(HIGH)
    main_rows = jnp.where(ends, 0.0, part).astype(LOW)

    shared_rows = gathered_over(shared_rows, FEAT[1])
    main_rows = gathered_over(main_rows, FEAT[1])
    shared_rows = gathered_over(shared_rows, FEAT[0])
    main_rows = gathered_over(main_rows, FEAT[0])
    other_rows = on_chip(shared_rows)
    other = on_chip(shared)

    errors = jnp.where(first, part, jnp.concatenate([other, shared], 1))

    grad_latent = contract_width(shared_rows, keep) + contract_width(other_rows, give)
    grad_latent = after(grad_latent)
    grad_latent = grad_latent + contract_width(main_rows, main)
    grad_pre = after((grad_latent * deriv).astype(LOW))
    total = lax.dot_general(inputs, grad_pre, (((0,), (0,)), ((), ())), preferred_element_type=HIGH)
    enc_grad = (total * tokens ** (-0.5)).astype(LOW)
    return (errors[None], enc_grad[None])


def solution(mesh):
    finer = Mesh(mesh.devices.reshape(mesh.shape["layer"], SIDE, SIDE), ("layer", *FEAT))
    in_specs = (
        P("layer", None, None),
        P("layer", FEAT, None),
        P("layer", None, FEAT),
        P("layer", FEAT),
        P("layer", FEAT, None, None),
        P("layer", None),
    )
    out_specs = (P("layer", FEAT, None), P("layer", None, FEAT))
    return jax.shard_map(local, mesh=finer, in_specs=in_specs, out_specs=out_specs, check_vma=False)
```

```python
import jax
import jax.numpy as jnp
from jax import lax
from jax.experimental import pallas as pl
from jax.experimental.pallas import tpu as pltpu
from jax.sharding import Mesh
from jax.sharding import PartitionSpec as P

FEAT = ("feat_0", "feat_1")
SIDE = 4
HIGH = jnp.float32
LOW = jnp.bfloat16


def exchanged(piece, axis, step):
    return lax.ppermute(piece, axis, [(i, i ^ step) for i in range(SIDE)])


def after(value, *others):
    return lax.optimization_barrier((value, *others))[0]


def sorted_kernel(blocks, decoder, rows, main, keep, give):
    first = lax.axis_index("layer") % 2 == 0
    half = keep.shape[1]

    @pl.when(pl.program_id(0) == 0)
    def _():
        x = lax.axis_index(FEAT[0])
        z = lax.axis_index(FEAT[1])
        for i in range(SIDE):
            for j in range(SIDE):
                rows[i * SIDE + j] = blocks[(x ^ i) * SIDE + (z ^ j)]

    planes = jnp.swapaxes(decoder[...], 0, 1)
    own = planes[0]
    later = planes[1]
    main[...] = jnp.where(first, own, later)
    keep[...] = jnp.where(first, later[:, :half], own[:, half:])
    give[...] = jnp.where(first, later[:, half:], own[:, :half])


def sorted_inputs(acts, decoder):
    tokens, width = acts.shape
    features = decoder.shape[0]
    blocks = acts.reshape(SIDE * SIDE, -1, width)
    tile = 256
    half = width // 2
    rows, main, keep, give = pl.pallas_call(
        sorted_kernel,
        grid=(features // tile,),
        in_specs=[
            pl.BlockSpec(blocks.shape, lambda n: (0, 0, 0)),
            pl.BlockSpec((tile, 2, width), lambda n: (n, 0, 0)),
        ],
        out_specs=[
            pl.BlockSpec(blocks.shape, lambda n: (0, 0, 0)),
            pl.BlockSpec((tile, width), lambda n: (n, 0)),
            pl.BlockSpec((tile, half), lambda n: (n, 0)),
            pl.BlockSpec((tile, half), lambda n: (n, 0)),
        ],
        out_shape=[
            jax.ShapeDtypeStruct(blocks.shape, acts.dtype),
            jax.ShapeDtypeStruct((features, width), decoder.dtype),
            jax.ShapeDtypeStruct((features, half), decoder.dtype),
            jax.ShapeDtypeStruct((features, half), decoder.dtype),
        ],
        compiler_params=pltpu.CompilerParams(vmem_limit_bytes=24 * 2**20),
        name="sorted_inputs",
    )(blocks, decoder)
    return rows.reshape(tokens, width), main, keep, give


def row_pieces(array):
    rows = array.shape[0] // SIDE
    return [array[i * rows : (i + 1) * rows] for i in range(SIDE)]


def received(pieces, axis):
    return [exchanged(pieces[step], axis, step) for step in range(1, SIDE)]


def totalled(piece, parts):
    total = piece.astype(HIGH)
    for part in parts:
        total = total + part.astype(HIGH)
    return total


def together(*values):
    return lax.optimization_barrier(values)


def on_chip(value):
    layers = lax.axis_size("layer")
    return lax.ppermute(value, "layer", [(i, i ^ 1) for i in range(layers)])


def across_chips(value):
    layers = lax.axis_size("layer")
    pairs = [(i, i + 1) for i in range(1, layers - 1, 2)]
    return lax.ppermute(value, "layer", pairs + [(j, i) for i, j in pairs])


def dot(a, b):
    return jnp.dot(a, b, preferred_element_type=HIGH)


def contract_width(errs, decoder):
    return lax.dot_general(errs, decoder, (((1,), (1,)), ((), ())), preferred_element_type=HIGH)


def local(acts, targets, enc_weight, enc_bias, dec_weight, dec_bias):
    weight = enc_weight[0]
    bias = enc_bias[0]
    decoder = dec_weight[0]
    tokens, width = acts.shape[1:]
    half = width // 2
    layer = lax.axis_index("layer")
    first = layer % 2 == 0
    ends = layer == lax.axis_size("layer") - 1

    inputs, main, keep, give = sorted_inputs(acts[0], decoder)

    pre = dot(inputs, weight) + bias
    scaled = 4.0 * pre
    small = jnp.exp(-jnp.abs(scaled))
    latent = ((jnp.maximum(scaled, 0.0) + jnp.log1p(small)) * 0.25).astype(LOW)
    latent, pre = lax.optimization_barrier((latent, pre))

    given, latent = together(dot(latent, give).astype(LOW), latent)
    given = on_chip(given)
    pieces = row_pieces(dot(latent, main).astype(LOW))
    pieces, latent, pre, lift, inputs = together(pieces, latent, pre, dec_bias[0], inputs)
    parts = received(pieces, FEAT[0])

    shared = (dot(latent, keep) + given.astype(HIGH)).astype(LOW)
    shared = shared.reshape(SIDE, SIDE, -1, half)
    side = together(*[shared[:, i].reshape(-1, half) for i in range(SIDE)])
    side_parts = received(side, FEAT[1])
    offset = lift - targets[0].astype(HIGH)
    peer_offset = on_chip(offset[:, :half])
    deriv, turned = together(jax.nn.sigmoid(4.0 * pre), inputs.T)

    piece, parts, side, side_parts, deriv, peer_offset, turned = together(
        pieces[0], parts, side[0], side_parts, deriv, peer_offset, turned
    )
    pieces = row_pieces(totalled(piece, parts).astype(LOW))
    side = row_pieces(totalled(side, side_parts).astype(LOW))

    pieces, side = together(pieces, side)
    parts = received(pieces, FEAT[1])
    side_parts = received(side, FEAT[0])

    piece, parts, side, side_parts = together(pieces[0], parts, side[0], side_parts)
    part = totalled(piece, parts) + jnp.where(first, offset, 0.0)
    shared = totalled(side, side_parts) + jnp.where(first, peer_offset, offset[:, half:])

    part, sent, shared, block = together(part, part.astype(LOW), shared, shared.astype(LOW))
    arrived = across_chips(sent)
    tiles = received([block] * SIDE, FEAT[1])
    other = on_chip(shared)

    part, arrived, block, tiles, other = together(part, arrived, block, tiles, other)
    part = part + arrived.astype(HIGH)
    rows = jnp.where(ends, 0.0, part).astype(LOW)
    block = jnp.concatenate([block, *tiles], 0)

    rows, block, part = together(rows, block, part)
    parts = received([rows] * SIDE, FEAT[1])
    tiles = received([block] * SIDE, FEAT[0])
    errors = jnp.where(first, part, jnp.concatenate([other, shared], 1))

    rows, parts, block, tiles, errors = together(rows, parts, block, tiles, errors)
    rows = jnp.concatenate([rows, *parts], 0)
    shared_rows = jnp.concatenate([block, *tiles], 0)

    rows, shared_rows = together(rows, shared_rows)
    parts = received([rows] * SIDE, FEAT[0])
    other_rows = on_chip(shared_rows)
    grad_latent = contract_width(shared_rows, keep) + contract_width(other_rows, give)

    grad_latent, rows, parts = together(grad_latent, rows, parts)
    main_rows = jnp.concatenate([rows, *parts], 0)
    grad_latent = grad_latent + contract_width(main_rows, main)
    grad_pre = after((grad_latent * deriv).astype(LOW))
    enc_grad = (dot(turned, grad_pre) * tokens ** (-0.5)).astype(LOW)
    return (errors[None], enc_grad[None])


def solution(mesh):
    finer = Mesh(mesh.devices.reshape(mesh.shape["layer"], SIDE, SIDE), ("layer", *FEAT))
    in_specs = (
        P("layer", None, None),
        P("layer", FEAT, None),
        P("layer", None, FEAT),
        P("layer", FEAT),
        P("layer", FEAT, None, None),
        P("layer", None),
    )
    out_specs = (P("layer", FEAT, None), P("layer", None, FEAT))
    return jax.shard_map(local, mesh=finer, in_specs=in_specs, out_specs=out_specs, check_vma=False)
```

```python
import jax
import jax.numpy as jnp
from jax import lax
from jax.experimental import pallas as pl
from jax.experimental.pallas import tpu as pltpu
from jax.sharding import Mesh
from jax.sharding import PartitionSpec as P

FEAT = ("feat_0", "feat_1")
SIDE = 4
STEPS = (0, 1, 3, 2)
HIGH = jnp.float32
LOW = jnp.bfloat16


def exchanged(piece, axis, step):
    return lax.ppermute(piece, axis, [(i, i ^ step) for i in range(SIDE)])


def after(value, *others):
    return lax.optimization_barrier((value, *others))[0]


def turned_kernel(blocks, rows):
    x = lax.axis_index(FEAT[0])
    z = lax.axis_index(FEAT[1])
    for i, step in enumerate(STEPS):
        for j, other in enumerate(STEPS):
            rows[i * SIDE + j] = blocks[(x ^ step) * SIDE + (z ^ other)]


def turned_tokens(acts):
    blocks = acts.reshape(SIDE * SIDE, -1, acts.shape[1])
    rows = pl.pallas_call(
        turned_kernel,
        in_specs=[pl.BlockSpec(memory_space=pltpu.VMEM)],
        out_specs=pl.BlockSpec(memory_space=pltpu.VMEM),
        out_shape=jax.ShapeDtypeStruct(blocks.shape, blocks.dtype),
        compiler_params=pltpu.CompilerParams(vmem_limit_bytes=8 * 2**20),
        name="turned_tokens",
    )(blocks)
    return rows.reshape(acts.shape)


def planes_kernel(decoder, main, keep, give):
    first = lax.axis_index("layer") % 2 == 0
    half = keep.shape[1]
    planes = jnp.swapaxes(decoder[...], 0, 1)
    own = planes[0]
    later = planes[1]
    main[...] = jnp.where(first, own, later)
    keep[...] = jnp.where(first, later[:, :half], own[:, half:])
    give[...] = jnp.where(first, later[:, half:], own[:, :half])


def split_planes(decoder):
    features, _, width = decoder.shape
    tile = 256
    half = width // 2
    return pl.pallas_call(
        planes_kernel,
        grid=(features // tile,),
        in_specs=[pl.BlockSpec((tile, 2, width), lambda n: (n, 0, 0))],
        out_specs=[
            pl.BlockSpec((tile, width), lambda n: (n, 0)),
            pl.BlockSpec((tile, half), lambda n: (n, 0)),
            pl.BlockSpec((tile, half), lambda n: (n, 0)),
        ],
        out_shape=[
            jax.ShapeDtypeStruct((features, width), decoder.dtype),
            jax.ShapeDtypeStruct((features, half), decoder.dtype),
            jax.ShapeDtypeStruct((features, half), decoder.dtype),
        ],
        compiler_params=pltpu.CompilerParams(vmem_limit_bytes=16 * 2**20),
        name="split_planes",
    )(decoder)


def row_pieces(array):
    rows = array.shape[0] // SIDE
    return [array[i * rows : (i + 1) * rows] for i in range(SIDE)]


def received(pieces, axis):
    return [exchanged(piece, axis, step) for piece, step in zip(pieces[1:], STEPS[1:])]


def totalled(piece, parts):
    total = piece.astype(HIGH)
    for part in parts:
        total = total + part.astype(HIGH)
    return total


def together(*values):
    return lax.optimization_barrier(values)


def on_chip(value):
    layers = lax.axis_size("layer")
    return lax.ppermute(value, "layer", [(i, i ^ 1) for i in range(layers)])


def across_chips(value):
    layers = lax.axis_size("layer")
    pairs = [(i, i + 1) for i in range(1, layers - 1, 2)]
    return lax.ppermute(value, "layer", pairs + [(j, i) for i, j in pairs])


def dot(a, b):
    return jnp.dot(a, b, preferred_element_type=HIGH)


def contract_width(errs, decoder):
    return lax.dot_general(errs, decoder, (((1,), (1,)), ((), ())), preferred_element_type=HIGH)


def local(acts, targets, enc_weight, enc_bias, dec_weight, dec_bias):
    weight = enc_weight[0]
    bias = enc_bias[0]
    decoder = dec_weight[0]
    tokens, width = acts.shape[1:]
    half = width // 2
    layer = lax.axis_index("layer")
    first = layer % 2 == 0
    ends = layer == lax.axis_size("layer") - 1

    inputs = turned_tokens(acts[0])
    offset = dec_bias[0] - targets[0].astype(HIGH)
    peer_offset = on_chip(offset[:, :half])

    pre = dot(inputs, weight) + bias
    scaled = 4.0 * pre
    small = jnp.exp(-jnp.abs(scaled))
    latent = ((jnp.maximum(scaled, 0.0) + jnp.log1p(small)) * 0.25).astype(LOW)
    latent, pre, decoder, peer_offset = together(latent, pre, decoder, peer_offset)
    main, keep, give = split_planes(decoder)

    given, latent = together(dot(latent, give).astype(LOW), latent)
    given = on_chip(given)
    pieces = row_pieces(dot(latent, main).astype(LOW))
    pieces, latent, pre, inputs = together(pieces, latent, pre, inputs)
    parts = received(pieces, FEAT[0])

    shared = (dot(latent, keep) + given.astype(HIGH)).astype(LOW)
    shared = shared.reshape(SIDE, SIDE, -1, half)
    side = together(*[shared[:, i].reshape(-1, half) for i in range(SIDE)])
    side_parts = received(side, FEAT[1])
    deriv, turned = together(jax.nn.sigmoid(4.0 * pre), inputs.T)

    piece, parts, side, side_parts, deriv, turned = together(
        pieces[0], parts, side[0], side_parts, deriv, turned
    )
    pieces = row_pieces(totalled(piece, parts).astype(LOW))
    side = row_pieces(totalled(side, side_parts).astype(LOW))

    pieces, side = together(pieces, side)
    parts = received(pieces, FEAT[1])
    side_parts = received(side, FEAT[0])

    piece, parts, side, side_parts = together(pieces[0], parts, side[0], side_parts)
    part = totalled(piece, parts) + jnp.where(first, offset, 0.0)
    shared = totalled(side, side_parts) + jnp.where(first, peer_offset, offset[:, half:])

    part, sent, shared, block = together(part, part.astype(LOW), shared, shared.astype(LOW))
    arrived = across_chips(sent)
    tiles = received([block] * SIDE, FEAT[1])

    part, arrived, block, tiles = together(part, arrived, block, tiles)
    part = part + arrived.astype(HIGH)
    rows = jnp.where(ends, 0.0, part).astype(LOW)
    block = jnp.concatenate([block, *tiles], 0)

    rows, block, part = together(rows, block, part)
    parts = received([rows] * SIDE, FEAT[1])
    tiles = received([block] * SIDE, FEAT[0])

    rows, parts, block, tiles = together(rows, parts, block, tiles)
    rows = jnp.concatenate([rows, *parts], 0)
    shared_rows = jnp.concatenate([block, *tiles], 0)

    rows, shared_rows, shared = together(rows, shared_rows, shared)
    near = [exchanged(rows, FEAT[0], 1), exchanged(rows, FEAT[0], 3)]
    other_rows = on_chip(shared_rows)
    other = on_chip(shared)
    grad_latent = contract_width(shared_rows, keep) + contract_width(other_rows, give)
    errors = jnp.where(first, part, jnp.concatenate([other, shared], 1))

    grad_latent, rows, near, errors = together(grad_latent, rows, near, errors)
    middle = rows.shape[0] // 2
    far = [exchanged(near[1][:middle], FEAT[0], 1), exchanged(near[0][middle:], FEAT[0], 3)]
    cut = tokens - rows.shape[0]
    early = jnp.concatenate([rows, *near], 0)
    grads = grad_latent[:cut] + contract_width(early, main)
    grads = after((grads * deriv[:cut]).astype(LOW))
    total = dot(turned[:, :cut], grads)

    total, far, grad_latent = together(total, far, grad_latent)
    grads = grad_latent[cut:] + contract_width(jnp.concatenate(far, 0), main)
    grads = after((grads * deriv[cut:]).astype(LOW))
    total = total + dot(turned[:, cut:], grads)
    enc_grad = (total * tokens ** (-0.5)).astype(LOW)
    return (errors[None], enc_grad[None])


def solution(mesh):
    finer = Mesh(mesh.devices.reshape(mesh.shape["layer"], SIDE, SIDE), ("layer", *FEAT))
    in_specs = (
        P("layer", None, None),
        P("layer", FEAT, None),
        P("layer", None, FEAT),
        P("layer", FEAT),
        P("layer", FEAT, None, None),
        P("layer", None),
    )
    out_specs = (P("layer", FEAT, None), P("layer", None, FEAT))
    return jax.shard_map(local, mesh=finer, in_specs=in_specs, out_specs=out_specs, check_vma=False)
```

```python
import jax
import jax.numpy as jnp
from jax import lax
from jax.experimental import pallas as pl
from jax.experimental.pallas import tpu as pltpu
from jax.sharding import Mesh
from jax.sharding import PartitionSpec as P

FEAT = ("feat_0", "feat_1")
SIDE = 4
STEPS = (0, 1, 3, 2)
HIGH = jnp.float32
LOW = jnp.bfloat16


def exchanged(piece, axis, step):
    return lax.ppermute(piece, axis, [(i, i ^ step) for i in range(SIDE)])


def after(value, *others):
    return lax.optimization_barrier((value, *others))[0]


def turned_kernel(blocks, rows):
    x = lax.axis_index(FEAT[0])
    z = lax.axis_index(FEAT[1])
    for i, step in enumerate(STEPS):
        for j, other in enumerate(STEPS):
            rows[i * SIDE + j] = blocks[(x ^ step) * SIDE + (z ^ other)]


def turned_tokens(acts):
    blocks = acts.reshape(SIDE * SIDE, -1, acts.shape[1])
    rows = pl.pallas_call(
        turned_kernel,
        in_specs=[pl.BlockSpec(memory_space=pltpu.VMEM)],
        out_specs=pl.BlockSpec(memory_space=pltpu.VMEM),
        out_shape=jax.ShapeDtypeStruct(blocks.shape, blocks.dtype),
        compiler_params=pltpu.CompilerParams(vmem_limit_bytes=8 * 2**20),
        name="turned_tokens",
    )(blocks)
    return rows.reshape(acts.shape)


def planes_kernel(decoder, main, keep, give):
    first = lax.axis_index("layer") % 2 == 0
    half = keep.shape[1]
    planes = jnp.swapaxes(decoder[...], 0, 1)
    own = planes[0]
    later = planes[1]
    main[...] = jnp.where(first, own, later)
    keep[...] = jnp.where(first, later[:, :half], own[:, half:])
    give[...] = jnp.where(first, later[:, half:], own[:, :half])


def split_planes(decoder):
    features, _, width = decoder.shape
    tile = 256
    half = width // 2
    return pl.pallas_call(
        planes_kernel,
        grid=(features // tile,),
        in_specs=[pl.BlockSpec((tile, 2, width), lambda n: (n, 0, 0))],
        out_specs=[
            pl.BlockSpec((tile, width), lambda n: (n, 0)),
            pl.BlockSpec((tile, half), lambda n: (n, 0)),
            pl.BlockSpec((tile, half), lambda n: (n, 0)),
        ],
        out_shape=[
            jax.ShapeDtypeStruct((features, width), decoder.dtype),
            jax.ShapeDtypeStruct((features, half), decoder.dtype),
            jax.ShapeDtypeStruct((features, half), decoder.dtype),
        ],
        compiler_params=pltpu.CompilerParams(vmem_limit_bytes=16 * 2**20),
        name="split_planes",
    )(decoder)


def row_pieces(array):
    rows = array.shape[0] // SIDE
    return [array[i * rows : (i + 1) * rows] for i in range(SIDE)]


def received(pieces, axis):
    return [exchanged(piece, axis, step) for piece, step in zip(pieces[1:], STEPS[1:])]


def totalled(piece, parts):
    total = piece.astype(HIGH)
    for part in parts:
        total = total + part.astype(HIGH)
    return total


def together(*values):
    return lax.optimization_barrier(values)


def on_chip(value):
    layers = lax.axis_size("layer")
    return lax.ppermute(value, "layer", [(i, i ^ 1) for i in range(layers)])


def across_chips(value):
    layers = lax.axis_size("layer")
    pairs = [(i, i + 1) for i in range(1, layers - 1, 2)]
    return lax.ppermute(value, "layer", pairs + [(j, i) for i, j in pairs])


def dot(a, b):
    return jnp.dot(a, b, preferred_element_type=HIGH)


def contract_width(errs, decoder):
    return lax.dot_general(errs, decoder, (((1,), (1,)), ((), ())), preferred_element_type=HIGH)


def local(acts, targets, enc_weight, enc_bias, dec_weight, dec_bias):
    weight = enc_weight[0]
    bias = enc_bias[0]
    decoder = dec_weight[0]
    tokens, width = acts.shape[1:]
    half = width // 2
    layer = lax.axis_index("layer")
    first = layer % 2 == 0
    ends = layer == lax.axis_size("layer") - 1

    inputs = turned_tokens(acts[0])

    pre = dot(inputs, weight) + bias
    scaled = 4.0 * pre
    small = jnp.exp(-jnp.abs(scaled))
    latent = ((jnp.maximum(scaled, 0.0) + jnp.log1p(small)) * 0.25).astype(LOW)
    latent, pre, decoder = together(latent, pre, decoder)
    main, keep, give = split_planes(decoder)

    given, latent = together(dot(latent, give).astype(LOW), latent)
    given = on_chip(given)
    pieces = row_pieces(dot(latent, main).astype(LOW))
    pieces, latent, pre, inputs = together(pieces, latent, pre, inputs)
    parts = received(pieces, FEAT[0])

    shared = (dot(latent, keep) + given.astype(HIGH)).astype(LOW)
    shared = shared.reshape(SIDE, SIDE, -1, half)
    side = together(*[shared[:, i].reshape(-1, half) for i in range(SIDE)])
    side, pre, inputs = together(side, pre, inputs)
    side_parts = received(side, FEAT[1])[::-1]
    deriv, turned, lift = together(jax.nn.sigmoid(4.0 * pre), inputs.T, dec_bias[0])
    offset = lift - targets[0].astype(HIGH)
    peer_offset = on_chip(offset[:, :half])

    side_parts, parts, piece, side, deriv, turned, peer_offset = together(
        side_parts, parts, pieces[0], side[0], deriv, turned, peer_offset
    )
    pieces = row_pieces(totalled(piece, parts).astype(LOW))
    side = row_pieces(totalled(side, side_parts).astype(LOW))

    pieces, side = together(pieces, side)
    parts = received(pieces, FEAT[1])[::-1]
    side_parts = received(side, FEAT[0])

    parts, piece, side, side_parts = together(parts, pieces[0], side[0], side_parts)
    part = totalled(piece, parts) + jnp.where(first, offset, 0.0)
    shared = totalled(side, side_parts) + jnp.where(first, peer_offset, offset[:, half:])

    part, sent, shared, block = together(part, part.astype(LOW), shared, shared.astype(LOW))
    arrived = across_chips(sent)
    tiles = received([block] * SIDE, FEAT[1])

    part, arrived, block, tiles = together(part, arrived, block, tiles)
    part = part + arrived.astype(HIGH)
    rows = jnp.where(ends, 0.0, part).astype(LOW)
    block = jnp.concatenate([block, *tiles], 0)

    rows, block, part = together(rows, block, part)
    parts = received([rows] * SIDE, FEAT[1])
    tiles = received([block] * SIDE, FEAT[0])

    rows, parts, block, tiles = together(rows, parts, block, tiles)
    rows = jnp.concatenate([rows, *parts], 0)
    shared_rows = jnp.concatenate([block, *tiles], 0)

    rows, shared_rows, shared = together(rows, shared_rows, shared)
    near = [exchanged(rows, FEAT[0], 1), exchanged(rows, FEAT[0], 3)]
    other_rows = on_chip(shared_rows)
    other = on_chip(shared)
    grad_latent = contract_width(shared_rows, keep) + contract_width(other_rows, give)
    errors = jnp.where(first, part, jnp.concatenate([other, shared], 1))

    grad_latent, rows, near, errors = together(grad_latent, rows, near, errors)
    middle = rows.shape[0] // 2
    far = [exchanged(near[1][:middle], FEAT[0], 1), exchanged(near[0][middle:], FEAT[0], 3)]
    cut = tokens - rows.shape[0]
    early = jnp.concatenate([rows, *near], 0)
    grads = grad_latent[:cut] + contract_width(early, main)
    grads = after((grads * deriv[:cut]).astype(LOW))
    total = dot(turned[:, :cut], grads)

    total, far, grad_latent = together(total, far, grad_latent)
    grads = grad_latent[cut:] + contract_width(jnp.concatenate(far, 0), main)
    grads = after((grads * deriv[cut:]).astype(LOW))
    total = total + dot(turned[:, cut:], grads)
    enc_grad = (total * tokens ** (-0.5)).astype(LOW)
    return (errors[None], enc_grad[None])


def solution(mesh):
    finer = Mesh(mesh.devices.reshape(mesh.shape["layer"], SIDE, SIDE), ("layer", *FEAT))
    in_specs = (
        P("layer", None, None),
        P("layer", FEAT, None),
        P("layer", None, FEAT),
        P("layer", FEAT),
        P("layer", FEAT, None, None),
        P("layer", None),
    )
    out_specs = (P("layer", FEAT, None), P("layer", None, FEAT))
    return jax.shard_map(local, mesh=finer, in_specs=in_specs, out_specs=out_specs, check_vma=False)
```

```python
import jax
import jax.numpy as jnp
from jax import lax
from jax.experimental import pallas as pl
from jax.experimental.pallas import tpu as pltpu
from jax.sharding import Mesh
from jax.sharding import PartitionSpec as P

FEAT = ("feat_0", "feat_1")
SIDE = 4
STEPS = (0, 1, 3, 2)
HIGH = jnp.float32
LOW = jnp.bfloat16


def exchanged(piece, axis, step):
    return lax.ppermute(piece, axis, [(i, i ^ step) for i in range(SIDE)])


def after(value, *others):
    return lax.optimization_barrier((value, *others))[0]


def turned_kernel(blocks, rows):
    x = lax.axis_index(FEAT[0])
    z = lax.axis_index(FEAT[1])
    for i, step in enumerate(STEPS):
        for j, other in enumerate(STEPS):
            rows[i * SIDE + j] = blocks[(x ^ step) * SIDE + (z ^ other)]


def turned_tokens(acts):
    blocks = acts.reshape(SIDE * SIDE, -1, acts.shape[1])
    rows = pl.pallas_call(
        turned_kernel,
        in_specs=[pl.BlockSpec(memory_space=pltpu.VMEM)],
        out_specs=pl.BlockSpec(memory_space=pltpu.VMEM),
        out_shape=jax.ShapeDtypeStruct(blocks.shape, blocks.dtype),
        compiler_params=pltpu.CompilerParams(vmem_limit_bytes=8 * 2**20),
        name="turned_tokens",
    )(blocks)
    return rows.reshape(acts.shape)


def planes_kernel(decoder, main, keep, give):
    first = lax.axis_index("layer") % 2 == 0
    half = keep.shape[1]
    planes = jnp.swapaxes(decoder[...], 0, 1)
    own = planes[0]
    later = planes[1]
    main[...] = jnp.where(first, own, later)
    keep[...] = jnp.where(first, later[:, :half], own[:, half:])
    give[...] = jnp.where(first, later[:, half:], own[:, :half])


def split_planes(decoder):
    features, _, width = decoder.shape
    tile = 256
    half = width // 2
    return pl.pallas_call(
        planes_kernel,
        grid=(features // tile,),
        in_specs=[pl.BlockSpec((tile, 2, width), lambda n: (n, 0, 0))],
        out_specs=[
            pl.BlockSpec((tile, width), lambda n: (n, 0)),
            pl.BlockSpec((tile, half), lambda n: (n, 0)),
            pl.BlockSpec((tile, half), lambda n: (n, 0)),
        ],
        out_shape=[
            jax.ShapeDtypeStruct((features, width), decoder.dtype),
            jax.ShapeDtypeStruct((features, half), decoder.dtype),
            jax.ShapeDtypeStruct((features, half), decoder.dtype),
        ],
        compiler_params=pltpu.CompilerParams(vmem_limit_bytes=16 * 2**20),
        name="split_planes",
    )(decoder)


def row_pieces(array):
    rows = array.shape[0] // SIDE
    return [array[i * rows : (i + 1) * rows] for i in range(SIDE)]


def received(pieces, axis):
    return [exchanged(piece, axis, step) for piece, step in zip(pieces[1:], STEPS[1:])]


def totalled(piece, parts):
    total = piece.astype(HIGH)
    for part in parts:
        total = total + part.astype(HIGH)
    return total


def together(*values):
    return lax.optimization_barrier(values)


def on_chip(value):
    layers = lax.axis_size("layer")
    return lax.ppermute(value, "layer", [(i, i ^ 1) for i in range(layers)])


def across_chips(value):
    layers = lax.axis_size("layer")
    pairs = [(i, i + 1) for i in range(1, layers - 1, 2)]
    return lax.ppermute(value, "layer", pairs + [(j, i) for i, j in pairs])


def dot(a, b):
    return jnp.dot(a, b, preferred_element_type=HIGH)


def contract_width(errs, decoder):
    return lax.dot_general(errs, decoder, (((1,), (1,)), ((), ())), preferred_element_type=HIGH)


def local(acts, targets, enc_weight, enc_bias, dec_weight, dec_bias):
    weight = enc_weight[0]
    bias = enc_bias[0]
    decoder = dec_weight[0]
    tokens, width = acts.shape[1:]
    half = width // 2
    layer = lax.axis_index("layer")
    first = layer % 2 == 0
    ends = layer == lax.axis_size("layer") - 1

    inputs = turned_tokens(acts[0])

    pre = dot(inputs, weight) + bias
    scaled = 4.0 * pre
    small = jnp.exp(-jnp.abs(scaled))
    latent = ((jnp.maximum(scaled, 0.0) + jnp.log1p(small)) * 0.25).astype(LOW)
    latent, pre, decoder = together(latent, pre, decoder)
    main, keep, give = split_planes(decoder)

    given, latent = together(dot(latent, give).astype(LOW), latent)
    given = on_chip(given)
    pieces = row_pieces(dot(latent, main).astype(LOW))
    pieces, latent, pre, inputs = together(pieces, latent, pre, inputs)
    parts = received(pieces, FEAT[0])

    shared = (dot(latent, keep) + given.astype(HIGH)).astype(LOW)
    shared = shared.reshape(SIDE, SIDE, -1, half)
    side = together(*[shared[:, i].reshape(-1, half) for i in range(SIDE)])
    side, pre, inputs = together(side, pre, inputs)
    side_parts = received(side, FEAT[1])[::-1]
    cut = tokens - tokens // SIDE
    deriv, *turned, lift = together(
        jax.nn.sigmoid(4.0 * pre), inputs[:cut].T, inputs[cut:].T, dec_bias[0]
    )
    offset = lift - targets[0].astype(HIGH)
    peer_offset = on_chip(offset[:, :half])

    side_parts, parts, piece, side, deriv, turned, peer_offset = together(
        side_parts, parts, pieces[0], side[0], deriv, turned, peer_offset
    )
    pieces = row_pieces(totalled(piece, parts).astype(LOW))
    side = row_pieces(totalled(side, side_parts).astype(LOW))

    pieces, side = together(pieces, side)
    parts = received(pieces, FEAT[1])[::-1]
    side_parts = received(side, FEAT[0])

    parts, piece, side, side_parts = together(parts, pieces[0], side[0], side_parts)
    part = totalled(piece, parts) + jnp.where(first, offset, 0.0)
    shared = totalled(side, side_parts) + jnp.where(first, peer_offset, offset[:, half:])

    part, sent, shared, block = together(part, part.astype(LOW), shared, shared.astype(LOW))
    arrived = across_chips(sent)
    tiles = received([block] * SIDE, FEAT[1])

    part, arrived, block, tiles = together(part, arrived, block, tiles)
    part = part + arrived.astype(HIGH)
    rows = jnp.where(ends, 0.0, part).astype(LOW)
    block = jnp.concatenate([block, *tiles], 0)

    rows, block, part = together(rows, block, part)
    parts = received([rows] * SIDE, FEAT[1])
    tiles = received([block] * SIDE, FEAT[0])

    rows, parts, block, tiles = together(rows, parts, block, tiles)
    rows = jnp.concatenate([rows, *parts], 0)
    shared_rows = jnp.concatenate([block, *tiles], 0)

    rows, shared_rows, shared = together(rows, shared_rows, shared)
    near = [exchanged(rows, FEAT[0], 1), exchanged(rows, FEAT[0], 3)]
    other_rows = on_chip(shared_rows)
    other = on_chip(shared)
    grad_latent = contract_width(shared_rows, keep) + contract_width(other_rows, give)
    errors = jnp.where(first, part, jnp.concatenate([other, shared], 1))

    grad_latent, rows, near, errors = together(grad_latent, rows, near, errors)
    middle = rows.shape[0] // 2
    far = [exchanged(near[1][:middle], FEAT[0], 1), exchanged(near[0][middle:], FEAT[0], 3)]
    early = jnp.concatenate([rows, *near], 0)
    grads = grad_latent[:cut] + contract_width(early, main)
    grads = after((grads * deriv[:cut]).astype(LOW))
    total = dot(turned[0], grads)

    total, far, grad_latent = together(total, far, grad_latent)
    grads = grad_latent[cut:] + contract_width(jnp.concatenate(far, 0), main)
    grads = after((grads * deriv[cut:]).astype(LOW))
    total = total + dot(turned[1], grads)
    enc_grad = (total * tokens ** (-0.5)).astype(LOW)
    return (errors[None], enc_grad[None])


def solution(mesh):
    finer = Mesh(mesh.devices.reshape(mesh.shape["layer"], SIDE, SIDE), ("layer", *FEAT))
    in_specs = (
        P("layer", None, None),
        P("layer", FEAT, None),
        P("layer", None, FEAT),
        P("layer", FEAT),
        P("layer", FEAT, None, None),
        P("layer", None),
    )
    out_specs = (P("layer", FEAT, None), P("layer", None, FEAT))
    return jax.shard_map(local, mesh=finer, in_specs=in_specs, out_specs=out_specs, check_vma=False)
```
